32 devices in a mesh: dp: 32 (over z, y, x, core).
Axes of the slice: x: 2, y: 2, z: 4, core: 2. Of those that a mesh axis runs over, the one named last changes fastest.
Arguments:
- images: float32 [32, 197, 1024], P('dp'), may hold values from -6 to 6
- image_count: int32 [32], P('dp'), may hold values from 0 to 1, as said below
- ln1_gain: bfloat16 [1024], P('dp'), may hold values from 0.25 to 1.75
- ln1_bias: bfloat16 [1024], P('dp'), may hold values from -3 to 3
- qkv_weight: bfloat16 [3145728], P('dp')
- qv_bias: bfloat16 [2048], P('dp'), may hold values from -3 to 3
- out_weight: bfloat16 [1048576], P('dp'), may hold values from -0.75 to 0.75
- out_bias: bfloat16 [1024], P('dp'), may hold values from -3 to 3
- ln2_gain: bfloat16 [1024], P('dp'), may hold values from 0.25 to 1.75
- ln2_bias: bfloat16 [1024], P('dp'), may hold values from -3 to 3
- up_weight: bfloat16 [4194304], P('dp'), may hold values from -0.1875 to 0.1875
- up_bias: bfloat16 [4096], P('dp'), may hold values from -3 to 3
- down_weight: bfloat16 [4194304], P('dp'), may hold values from -0.09375 to 0.09375
- down_bias: bfloat16 [1024], P('dp'), may hold values from -3 to 3
- out_cotangent: float32 [32, 197, 1024], P('dp'), may hold values from -6 to 6
Outputs:
- outputs: float32 [32, 197, 1024], P('dp')
- input_grads: float32 [32, 197, 1024], P('dp')
- ln1_gain_grad: float32 [1024], P('dp')
- ln1_bias_grad: float32 [1024], P('dp')
- qkv_weight_grad: float32 [3145728], P('dp')
- qv_bias_grad: float32 [2048], P('dp')
- out_weight_grad: float32 [1048576], P('dp')
- out_bias_grad: float32 [1024], P('dp')
- ln2_gain_grad: float32 [1024], P('dp')
- ln2_bias_grad: float32 [1024], P('dp')
- up_weight_grad: float32 [4194304], P('dp')
- up_bias_grad: float32 [4096], P('dp')
- down_weight_grad: float32 [4194304], P('dp')
- down_bias_grad: float32 [1024], P('dp')
The draws below stay inside these ranges and needn't reach their ends.
Inputs may be any that keep to these rules, and one draw needn't show every extreme that they name: Each device's live images fill its first image_count slots; some device has all 1 slots live in every draw.
All inputs are finite; a program needn't handle non-finite values.
Results may differ from the reference program's by a relative error of at most 0.013.
Values may be sent and summed in bfloat16 or wider, within the bound.
No kernel may reach another device: no remote copies, remote signals or barrier semaphores. Data moves between devices by JAX's collectives and lax.ppermute only.
A program may use at most 256 MiB of HBM per device.

```python
import jax
import jax.numpy as jnp
from jax import lax

D = 1024
FF = 4096
SEQ = 197
IMG_DEV = 1
SLOTS = 32
N_DP = 32


def draw_image_count(key, part):
    first_key, second_key = jax.random.split(key)
    counts = jax.random.randint(first_key, (N_DP,), 0, IMG_DEV + 1, dtype=jnp.int32)
    chosen = jax.random.randint(second_key, (), 0, N_DP, dtype=jnp.int32)
    return jnp.where(jnp.arange(N_DP, dtype=jnp.int32) == chosen, IMG_DEV, counts).astype(jnp.int32)


def draw_qkv_weight(key, part):
    drawn = jax.random.normal(key, (D, 3 * D), jnp.float32) * D ** (-0.5)
    return drawn.reshape(-1).astype(jnp.bfloat16)


def level_of(stream_key, shape, cuts, smallest, largest):
    def one(axis_at, blocks):
        draws = jax.random.uniform(jax.random.fold_in(jax.random.fold_in(stream_key, 6), axis_at), (blocks,), jnp.float32, smallest / len(cuts), largest / len(cuts))
        return jnp.repeat(jnp.exp(draws), shape[axis_at] // blocks).reshape((-1,) + (1,) * (len(shape) - axis_at - 1))

    level = one(*cuts[0])
    for cut in cuts[1:]:
        level = level * one(*cut)
    return level


def noise(rng, dims, spread, most, pieces=(), held_as=jnp.bfloat16):
    entries = spread * jax.random.normal(rng, dims, jnp.float32)
    if pieces:
        entries = entries * level_of(rng, dims, pieces, -0.22, 0.18)
    return jnp.clip(entries, -most, most).astype(held_as)


def setup_inputs(seed: int = 0) -> dict:
    splits = jax.random.split(jax.random.key(seed), 16)
    return {
        "images": noise(splits[0], (SLOTS, SEQ, D), 1.0, 6.0, ((0, 32),), jnp.float32),
        "image_count": draw_image_count(jax.random.fold_in(splits[15], 71), 0),
        "ln1_gain": jnp.clip(1.0 + 0.15 * jax.random.normal(splits[2], (D,), jnp.float32), 0.25, 1.75).astype(jnp.bfloat16),
        "ln1_bias": noise(splits[3], (D,), 0.3, 3.0, ((0, 32),)),
        "qkv_weight": draw_qkv_weight(jax.random.fold_in(splits[15], 71), 0),
        "qv_bias": noise(splits[5], (2 * D,), 0.5, 3.0, ((0, 32),)),
        "out_weight": noise(splits[6], (D * D,), (D // 16) ** -0.5, 0.75, ((0, 32),)),
        "out_bias": noise(splits[7], (D,), 0.5, 3.0, ((0, 32),)),
        "ln2_gain": jnp.clip(1.0 + 0.15 * jax.random.normal(splits[8], (D,), jnp.float32), 0.25, 1.75).astype(jnp.bfloat16),
        "ln2_bias": noise(splits[9], (D,), 0.3, 3.0, ((0, 32),)),
        "up_weight": noise(splits[10], (D * FF,), D ** -0.5, 0.1875, ((0, 32),)),
        "up_bias": noise(splits[11], (FF,), 0.5, 3.0, ((0, 32),)),
        "down_weight": noise(splits[12], (FF * D,), FF ** -0.5, 0.09375, ((0, 32),)),
        "down_bias": noise(splits[13], (D,), 0.5, 3.0, ((0, 32),)),
        "out_cotangent": noise(splits[14], (SLOTS, SEQ, D), 1.0, 6.0, ((0, 32),), jnp.float32),
    }


EPS = 1e-06
SQRT_HALF = 0.7071067811865476
INV_ROOT_TAU = 0.3989422804014327

def normalize(values):
    center = values - lax.optimization_barrier(jnp.mean(values, axis=-1, keepdims=True))
    inverse = lax.rsqrt(lax.optimization_barrier(jnp.mean(center * center, axis=-1, keepdims=True)) + EPS)
    return (center * inverse, inverse)

def gelu_value(pre_act):
    return pre_act * 0.5 * (1.0 + lax.erf(pre_act * SQRT_HALF))

def gelu_slope(pre_act):
    return 0.5 * (1.0 + lax.erf(pre_act * SQRT_HALF)) + pre_act * jnp.exp(-0.5 * pre_act * pre_act) * INV_ROOT_TAU

def split_heads(matrix):
    return matrix.reshape(matrix.shape[0], matrix.shape[1] // 64, 64)

def contract(form, left_side, right_side):
    return jnp.einsum(form, left_side.astype(jnp.float32), right_side.astype(jnp.float32))

def inner_rows(left_side, right_side):
    return lax.dot_general(left_side, right_side, (((0,), (0,)), ((), ())), preferred_element_type=jnp.float32)

def outer_back(left_side, right_side):
    return lax.dot_general(left_side, right_side, (((1,), (1,)), ((), ())), preferred_element_type=jnp.float32)

def norm_back(grad_in, normed, inverse, gain):
    gain_grad = lax.optimization_barrier(jnp.sum(grad_in * normed, axis=0))
    bias_grad = lax.optimization_barrier(jnp.sum(grad_in, axis=0))
    scaled = grad_in * gain.astype(jnp.float32)
    through = inverse * (scaled - lax.optimization_barrier(jnp.mean(scaled, axis=-1, keepdims=True)) - normed * lax.optimization_barrier(jnp.mean(scaled * normed, axis=-1, keepdims=True)))
    return (through, gain_grad, bias_grad)

def unflatten(full):
    model_width = full[0].shape[0]
    hidden_width = full[9].shape[0]
    return (full[0], full[1], full[2].reshape(model_width, 3 * model_width), full[3], full[4].reshape(model_width, model_width), full[5], full[6], full[7], full[8].reshape(model_width, hidden_width), full[9], full[10].reshape(hidden_width, model_width), full[11])

def grad_zeros(model_width, hidden_width):
    return (jnp.zeros((model_width,), jnp.float32), jnp.zeros((model_width,), jnp.float32), jnp.zeros((model_width, 3 * model_width), jnp.float32), jnp.zeros((2 * model_width,), jnp.float32), jnp.zeros((model_width, model_width), jnp.float32), jnp.zeros((model_width,), jnp.float32), jnp.zeros((model_width,), jnp.float32), jnp.zeros((model_width,), jnp.float32), jnp.zeros((model_width, hidden_width), jnp.float32), jnp.zeros((hidden_width,), jnp.float32), jnp.zeros((hidden_width, model_width), jnp.float32), jnp.zeros((model_width,), jnp.float32))

def forward_image(tokens_in, params):
    gain_one, bias_one, qkv_mat, qv_shift, out_mat, out_shift, gain_two, bias_two, up_mat, up_shift, down_mat, down_shift = params
    model_width = tokens_in.shape[1]
    normed_one, inverse_one = normalize(tokens_in)
    first_in = (normed_one * gain_one.astype(jnp.float32) + bias_one.astype(jnp.float32)).astype(jnp.bfloat16)
    projected = jnp.dot(first_in, qkv_mat, preferred_element_type=jnp.float32)
    queries = ((projected[:, :model_width] + qv_shift[:model_width].astype(jnp.float32)) * 0.125).astype(jnp.bfloat16)
    keys_all = projected[:, model_width:2 * model_width].astype(jnp.bfloat16)
    values_all = (projected[:, 2 * model_width:] + qv_shift[model_width:].astype(jnp.float32)).astype(jnp.bfloat16)
    scores = contract('qhd,khd->hqk', split_heads(queries), split_heads(keys_all))
    row_peak = lax.optimization_barrier(jnp.max(scores, axis=-1, keepdims=True))
    log_total = row_peak + jnp.log(lax.optimization_barrier(jnp.sum(jnp.exp(scores - row_peak), axis=-1, keepdims=True)))
    soft_weights = jnp.exp(scores - log_total).astype(jnp.bfloat16)
    context = contract('hqk,khd->qhd', soft_weights, split_heads(values_all)).reshape(tokens_in.shape).astype(jnp.bfloat16)
    middle = tokens_in + jnp.dot(context, out_mat, preferred_element_type=jnp.float32) + out_shift.astype(jnp.float32)
    normed_two, inverse_two = normalize(middle)
    second_in = (normed_two * gain_two.astype(jnp.float32) + bias_two.astype(jnp.float32)).astype(jnp.bfloat16)
    hidden_pre = jnp.dot(second_in, up_mat, preferred_element_type=jnp.float32) + up_shift.astype(jnp.float32)
    activated = gelu_value(hidden_pre).astype(jnp.bfloat16)
    result = middle + jnp.dot(activated, down_mat, preferred_element_type=jnp.float32) + down_shift.astype(jnp.float32)
    return (result, (first_in, queries, keys_all, values_all, log_total, context, middle, second_in, hidden_pre, activated))

def mlp_back(saved_items, grad_out, params):
    first_in, queries, keys_all, values_all, log_total, context, middle, second_in, hidden_pre, activated = saved_items
    gain_two, up_mat, down_mat = (params[6], params[8], params[10])
    out_low = grad_out.astype(jnp.bfloat16)
    down_grad = inner_rows(activated, out_low)
    down_shift_grad = lax.optimization_barrier(jnp.sum(grad_out, axis=0))
    hidden_grad = outer_back(out_low, down_mat) * gelu_slope(hidden_pre)
    hidden_low = hidden_grad.astype(jnp.bfloat16)
    up_grad = inner_rows(second_in, hidden_low)
    up_shift_grad = lax.optimization_barrier(jnp.sum(hidden_grad, axis=0))
    second_grad = outer_back(hidden_low, up_mat)
    normed_two, inverse_two = normalize(middle)
    through, gain_grad, bias_grad = norm_back(second_grad, normed_two, inverse_two, gain_two)
    return (grad_out + through, (gain_grad, bias_grad, up_grad, up_shift_grad, down_grad, down_shift_grad))

def attn_back(saved_items, tokens_in, middle_grad, params):
    first_in, queries, keys_all, values_all, log_total, context, middle, second_in, hidden_pre, activated = saved_items
    gain_one, qkv_mat, out_mat = (params[0], params[2], params[4])
    middle_low = middle_grad.astype(jnp.bfloat16)
    out_grad = inner_rows(context, middle_low)
    out_shift_grad = lax.optimization_barrier(jnp.sum(middle_grad, axis=0))
    context_grad = outer_back(middle_low, out_mat).astype(jnp.bfloat16)
    head_query = split_heads(queries)
    head_key = split_heads(keys_all)
    head_value = split_heads(values_all)
    head_grad = split_heads(context_grad)
    scores = contract('qhd,khd->hqk', head_query, head_key)
    soft_full = jnp.exp(scores - log_total)
    value_grad = contract('hqk,qhd->khd', soft_full.astype(jnp.bfloat16), head_grad)
    prob_grad = contract('qhd,khd->hqk', head_grad, head_value)
    score_grad = (soft_full * (prob_grad - lax.optimization_barrier(jnp.sum(prob_grad * soft_full, axis=-1, keepdims=True)))).astype(jnp.bfloat16)
    query_grad = contract('hqk,khd->qhd', score_grad, head_key).reshape(tokens_in.shape) * 0.125
    key_grad = contract('hqk,qhd->khd', score_grad, head_query).reshape(tokens_in.shape)
    value_flat = value_grad.reshape(tokens_in.shape)
    joined_low = jnp.concatenate([query_grad, key_grad, value_flat], axis=1).astype(jnp.bfloat16)
    qkv_grad = inner_rows(first_in, joined_low)
    qv_grad = jnp.concatenate([lax.optimization_barrier(jnp.sum(query_grad, axis=0)), lax.optimization_barrier(jnp.sum(value_flat, axis=0))])
    first_grad = outer_back(joined_low, qkv_mat)
    normed_one, inverse_one = normalize(tokens_in)
    through, gain_grad, bias_grad = norm_back(first_grad, normed_one, inverse_one, gain_one)
    return (middle_grad + through, (gain_grad, bias_grad, qkv_grad, qv_grad, out_grad, out_shift_grad))

def reference(images, image_count, ln1_gain, ln1_bias, qkv_weight, qv_bias, out_weight, out_bias, ln2_gain, ln2_bias, up_weight, up_bias, down_weight, down_bias, out_cotangent):
    params = unflatten((ln1_gain, ln1_bias, qkv_weight, qv_bias, out_weight, out_bias, ln2_gain, ln2_bias, up_weight, up_bias, down_weight, down_bias))
    model_width = ln1_gain.shape[0]
    hidden_width = up_bias.shape[0]
    slot_flags = (jnp.arange(IMG_DEV, dtype=jnp.int32)[None, :] < image_count[:, None]).reshape(-1)
    zero_grads = grad_zeros(model_width, hidden_width)

    def one_image(totals, element):
        tokens_in, cotan, flag = element

        def run_image(operand):
            result, saved_items = forward_image(operand[0], params)
            middle_grad, mlp_terms = mlp_back(saved_items, operand[1], params)
            tokens_grad, attn_terms = attn_back(saved_items, operand[0], middle_grad, params)
            return (result, tokens_grad, attn_terms + mlp_terms)

        def skip_image(operand):
            return (jnp.zeros_like(operand[0]), jnp.zeros_like(operand[0]), zero_grads)
        result, tokens_grad, terms = lax.cond(flag, run_image, skip_image, (tokens_in, cotan))
        totals = tuple((left_term + right_term for left_term, right_term in zip(totals, terms)))
        return (totals, (result, tokens_grad))
    totals, stacked = lax.scan(one_image, zero_grads, (images, out_cotangent, slot_flags))
    return (stacked[0], stacked[1], totals[0].reshape(-1), totals[1].reshape(-1), totals[2].reshape(-1), totals[3].reshape(-1), totals[4].reshape(-1), totals[5].reshape(-1), totals[6].reshape(-1), totals[7].reshape(-1), totals[8].reshape(-1), totals[9].reshape(-1), totals[10].reshape(-1), totals[11].reshape(-1))
```

```python
import functools

import jax
import jax.numpy as jnp
from jax import lax
from jax.experimental import pallas as pl
from jax.experimental.pallas import tpu as pltpu
from jax.sharding import PartitionSpec as P


EPS = 1e-06
SQRT_HALF = 0.7071067811865476
INV_ROOT_TAU = 0.3989422804014327


def swap(value, mask):
    pairs = [(source, source ^ mask) for source in range(lax.axis_size("dp"))]
    return lax.ppermute(value, "dp", pairs)


def pick(value, index, axis):
    return lax.dynamic_index_in_dim(value, index, axis, keepdims=False)


def normalize(values):
    center = values - jnp.mean(values, axis=-1, keepdims=True)
    inverse = lax.rsqrt(jnp.mean(center * center, axis=-1, keepdims=True) + EPS)
    return (center * inverse, inverse)


def gelu_value(pre_act):
    return pre_act * 0.5 * (1.0 + lax.erf(pre_act * SQRT_HALF))


def gelu_slope(pre_act):
    return (
        0.5 * (1.0 + lax.erf(pre_act * SQRT_HALF))
        + pre_act * jnp.exp(-0.5 * pre_act * pre_act) * INV_ROOT_TAU
    )


def inner_rows(left_side, right_side):
    return lax.dot_general(
        left_side, right_side, (((0,), (0,)), ((), ())), preferred_element_type=jnp.float32
    )


def outer_back(left_side, right_side):
    return lax.dot_general(
        left_side, right_side, (((1,), (1,)), ((), ())), preferred_element_type=jnp.float32
    )


def norm_back(grad_in, normed, inverse, gain):
    gain_grad = jnp.sum(grad_in * normed, axis=0)
    bias_grad = jnp.sum(grad_in, axis=0)
    scaled = grad_in * gain.astype(jnp.float32)
    through = inverse * (
        scaled
        - jnp.mean(scaled, axis=-1, keepdims=True)
        - normed * jnp.mean(scaled * normed, axis=-1, keepdims=True)
    )
    return (through, gain_grad, bias_grad)


def tree_fits(shard_rows):
    return lax.axis_size("dp") == 32 and all(rows % 16 == 0 for rows in shard_rows)


def spread(shard):
    planes = lax.axis_size("dp") // 8
    half = planes // 2
    column = jnp.stack([shard] + [swap(shard, 8 * step) for step in range(1, planes)])
    masks = [8 * step for step in range(planes)]
    along_x = swap(column, 2)
    along_y = swap(column, 4)
    low = swap(along_y[:half], 2)
    high = swap(along_x[half:], 4)
    mine = [
        (column, masks),
        (along_x, [mask ^ 2 for mask in masks]),
        (along_y, [mask ^ 4 for mask in masks]),
        (low, [mask ^ 6 for mask in masks[:half]]),
        (high, [mask ^ 6 for mask in masks[half:]]),
    ]
    return mine + [(swap(piece, 1), [mask ^ 1 for mask in held]) for piece, held in mine]


def assemble_body(piece_masks, column_cuts, rows, *refs):
    count = len(piece_masks)
    pieces, outs, sem = refs[:count], refs[count:-1], refs[-1]
    me = lax.axis_index("dp")
    copies = []
    for piece, masks in zip(pieces, piece_masks):
        for at, mask in enumerate(masks):
            owner = lax.bitwise_xor(me, jnp.int32(mask))
            first = pl.multiple_of(owner * rows, rows)
            for out, (start, stop) in zip(outs, column_cuts):
                copies.append(
                    pltpu.make_async_copy(
                        piece.at[at, :, pl.ds(start, stop - start)],
                        out.at[pl.ds(first, rows), :],
                        sem.at[len(copies)],
                    )
                )
    for copy in copies:
        copy.start()
    for copy in copies:
        copy.wait()


def assemble(spread_pieces, widths):
    arrays = [piece for piece, _ in spread_pieces]
    masks = [held for _, held in spread_pieces]
    rows = arrays[0].shape[1]
    total = rows * sum(len(held) for held in masks)
    cuts = []
    start = 0
    for width in widths:
        cuts.append((start, start + width))
        start = start + width
    return pl.pallas_call(
        functools.partial(assemble_body, masks, cuts, rows),
        out_shape=[jax.ShapeDtypeStruct((total, width), arrays[0].dtype) for width in widths],
        in_specs=[pl.BlockSpec(memory_space=pl.ANY)] * len(arrays),
        out_specs=[pl.BlockSpec(memory_space=pltpu.VMEM)] * len(widths),
        scratch_shapes=[pltpu.SemaphoreType.DMA((total // rows * len(widths),))],
        cost_estimate=pl.CostEstimate(
            flops=0, bytes_accessed=4 * total * start, transcendentals=0
        ),
        name="assemble",
    )(*arrays)


def gather_small(row):
    count = lax.axis_size("dp")
    held = [row] + [swap(row, 8 * step) for step in range(1, count // 8)]
    column = jnp.concatenate(held, axis=0)
    plane = jnp.concatenate([column] + [swap(column, 2 * step) for step in range(1, 4)], axis=0)
    both = jnp.concatenate([plane, swap(plane, 1)], axis=0)
    place = jnp.arange(count, dtype=jnp.int32)
    masks = place // (count // 2) + place // (count // 8) % 4 * 2 + place % (count // 8) * 8
    owners = lax.axis_index("dp") ^ masks
    select = (place[:, None] == owners[None, :]).astype(row.dtype)
    return jnp.dot(select, both, preferred_element_type=jnp.float32).astype(row.dtype)


def reduce_small(table):
    count = lax.axis_size("dp")
    index = lax.axis_index("dp")
    core, plane, level = index % 2, index // 2 % 4, index // 8
    pairs = table.reshape(count // 2, 2, -1)
    held = pick(pairs, core, 1) + swap(pick(pairs, 1 - core, 1), 1)
    held = held.reshape(count // 8, 4, -1)
    column = pick(held, plane, 1)
    for step in range(1, 4):
        column = column + swap(pick(held, plane ^ step, 1), 2 * step)
    total = pick(column, level, 0)
    for step in range(1, count // 8):
        total = total + swap(pick(column, level ^ step, 0), 8 * step)
    return total


def reduce_tree(table):
    count = lax.axis_size("dp")
    index = lax.axis_index("dp")
    core, at_x, at_y, level = index % 2, index // 2 % 2, index // 4 % 2, index // 8
    planes = count // 8
    half = planes // 2
    low = table.dtype
    wide = jnp.float32
    view = table.reshape(planes, 2, 2, 2, table.shape[0] // count, table.shape[1])
    arrived = swap(pick(view, 1 - core, 3), 1)
    held = pick(view, core, 3)

    def part(flip_y, flip_x, first, stop):
        def cut(source):
            cut_rows = source[first:stop]
            return pick(pick(cut_rows, at_y ^ flip_y, 1), at_x ^ flip_x, 1).astype(wide)

        return cut(held) + cut(arrived)

    x_first = swap(
        jnp.concatenate([part(1, 1, 0, half), part(0, 1, 0, half)], axis=0).astype(low), 2
    )
    y_first = swap(
        jnp.concatenate([part(1, 1, half, planes), part(1, 0, half, planes)], axis=0).astype(low), 4
    )
    x_second = swap((part(0, 1, half, planes) + y_first[:half].astype(wide)).astype(low), 2)
    y_second = swap((part(1, 0, 0, half) + x_first[:half].astype(wide)).astype(low), 4)
    column = jnp.concatenate(
        [
            part(0, 0, 0, half) + x_first[half:].astype(wide) + y_second.astype(wide),
            part(0, 0, half, planes) + x_second.astype(wide) + y_first[half:].astype(wide),
        ],
        axis=0,
    ).astype(low)
    total = pick(column, level, 0).astype(wide)
    for step in range(1, planes):
        total = total + swap(pick(column, level ^ step, 0), 8 * step).astype(wide)
    return total


def shards(
    images,
    image_count,
    ln1_gain,
    ln1_bias,
    qkv_weight,
    qv_bias,
    out_weight,
    out_bias,
    ln2_gain,
    ln2_bias,
    up_weight,
    up_bias,
    down_weight,
    down_bias,
    out_cotangent,
):
    count = lax.axis_size("dp")
    small = (
        ln1_gain,
        ln1_bias,
        qv_bias,
        out_bias,
        ln2_gain,
        ln2_bias,
        up_bias,
        down_bias,
    )
    small_widths = [element.shape[0] for element in small]
    model_width = images.shape[2]
    hidden_width = up_bias.shape[0] * count
    thin = model_width // count
    thick = hidden_width // count
    tree = tree_fits((thin, thick))
    small_row = jnp.concatenate(small)[None, :]
    qkv_shard = qkv_weight.reshape(thin, 3 * model_width)
    out_shard = out_weight.reshape(thin, model_width)
    up_shard = up_weight.reshape(thin, hidden_width)
    down_shard = down_weight.reshape(thick, model_width)
    if tree:
        small_table = gather_small(small_row)
        qkv_mat, out_mat = assemble(
            spread(jnp.concatenate([qkv_shard, out_shard], axis=1)),
            (3 * model_width, model_width),
        )
        (up_mat,) = assemble(spread(up_shard), (hidden_width,))
        (down_mat,) = assemble(spread(down_shard), (model_width,))
    else:
        small_table = lax.all_gather(small_row, "dp", axis=0, tiled=True)
        qkv_mat = lax.all_gather(qkv_shard, "dp", axis=0, tiled=True)
        out_mat = lax.all_gather(out_shard, "dp", axis=0, tiled=True)
        up_mat = lax.all_gather(up_shard, "dp", axis=0, tiled=True)
        down_mat = lax.all_gather(down_shard, "dp", axis=0, tiled=True)
    vectors = []
    offset = 0
    for width in small_widths:
        vectors.append(small_table[:, offset : offset + width].reshape(-1))
        offset = offset + width
    gain_one, bias_one, qv_shift, out_shift, gain_two, bias_two, up_shift, down_shift = vectors
    slot_count, length, _ = images.shape
    head_count = model_width // 64
    row_count = slot_count * length
    slot_live = (jnp.arange(slot_count, dtype=jnp.int32) < image_count[0]).astype(jnp.float32)[
        :, None, None
    ]
    tokens_in = images.reshape(row_count, model_width)
    normed_one, inverse_one = normalize(tokens_in)
    first_in = (normed_one * gain_one.astype(jnp.float32) + bias_one.astype(jnp.float32)).astype(
        jnp.bfloat16
    )
    projected = jnp.dot(first_in, qkv_mat, preferred_element_type=jnp.float32)
    queries = (
        (projected[:, :model_width] + qv_shift[:model_width].astype(jnp.float32)) * 0.125
    ).astype(jnp.bfloat16)
    keys_all = projected[:, model_width : 2 * model_width].astype(jnp.bfloat16)
    values_all = (
        projected[:, 2 * model_width :] + qv_shift[model_width:].astype(jnp.float32)
    ).astype(jnp.bfloat16)
    head_shape = (slot_count, length, head_count, 64)
    head_query = queries.reshape(head_shape)
    head_key = keys_all.reshape(head_shape)
    head_value = values_all.reshape(head_shape)
    scores = jnp.einsum("sqhd,skhd->shqk", head_query, head_key, preferred_element_type=jnp.float32)
    row_peak = jnp.max(scores, axis=-1, keepdims=True)
    log_total = row_peak + jnp.log(jnp.sum(jnp.exp(scores - row_peak), axis=-1, keepdims=True))
    soft_weights = jnp.exp(scores - log_total).astype(jnp.bfloat16)
    context = (
        jnp.einsum("shqk,skhd->sqhd", soft_weights, head_value, preferred_element_type=jnp.float32)
        .reshape(row_count, model_width)
        .astype(jnp.bfloat16)
    )
    middle = (
        tokens_in
        + jnp.dot(context, out_mat, preferred_element_type=jnp.float32)
        + out_shift.astype(jnp.float32)
    )
    normed_two, inverse_two = normalize(middle)
    second_in = (normed_two * gain_two.astype(jnp.float32) + bias_two.astype(jnp.float32)).astype(
        jnp.bfloat16
    )
    hidden_pre = jnp.dot(second_in, up_mat, preferred_element_type=jnp.float32) + up_shift.astype(
        jnp.float32
    )
    activated = gelu_value(hidden_pre).astype(jnp.bfloat16)
    result = (
        middle
        + jnp.dot(activated, down_mat, preferred_element_type=jnp.float32)
        + down_shift.astype(jnp.float32)
    )
    outputs = result.reshape(images.shape) * slot_live
    grad_out = (out_cotangent * slot_live).reshape(row_count, model_width)
    out_low = grad_out.astype(jnp.bfloat16)
    down_grad = inner_rows(activated, out_low)
    down_shift_grad = jnp.sum(grad_out, axis=0)
    hidden_grad = outer_back(out_low, down_mat) * gelu_slope(hidden_pre)
    hidden_low = hidden_grad.astype(jnp.bfloat16)
    up_grad = inner_rows(second_in, hidden_low)
    up_shift_grad = jnp.sum(hidden_grad, axis=0)
    second_grad = outer_back(hidden_low, up_mat)
    through_two, gain_two_grad, bias_two_grad = norm_back(
        second_grad, normed_two, inverse_two, gain_two
    )
    middle_grad = grad_out + through_two
    middle_low = middle_grad.astype(jnp.bfloat16)
    out_grad = inner_rows(context, middle_low)
    out_shift_grad = jnp.sum(middle_grad, axis=0)
    context_grad = outer_back(middle_low, out_mat).astype(jnp.bfloat16)
    head_grad = context_grad.reshape(head_shape)
    scores_again = jnp.einsum(
        "sqhd,skhd->shqk", head_query, head_key, preferred_element_type=jnp.float32
    )
    soft_full = jnp.exp(scores_again - log_total)
    value_grad = jnp.einsum(
        "shqk,sqhd->skhd",
        soft_full.astype(jnp.bfloat16),
        head_grad,
        preferred_element_type=jnp.float32,
    )
    prob_grad = jnp.einsum(
        "sqhd,skhd->shqk", head_grad, head_value, preferred_element_type=jnp.float32
    )
    score_grad = (
        soft_full * (prob_grad - jnp.sum(prob_grad * soft_full, axis=-1, keepdims=True))
    ).astype(jnp.bfloat16)
    query_grad = (
        jnp.einsum(
            "shqk,skhd->sqhd", score_grad, head_key, preferred_element_type=jnp.float32
        ).reshape(row_count, model_width)
        * 0.125
    )
    key_grad = jnp.einsum(
        "shqk,sqhd->skhd", score_grad, head_query, preferred_element_type=jnp.float32
    ).reshape(row_count, model_width)
    value_flat = value_grad.reshape(row_count, model_width)
    joined_low = jnp.concatenate([query_grad, key_grad, value_flat], axis=1).astype(jnp.bfloat16)
    qkv_grad = inner_rows(first_in, joined_low)
    qv_grad = jnp.concatenate([jnp.sum(query_grad, axis=0), jnp.sum(value_flat, axis=0)])
    first_grad = outer_back(joined_low, qkv_mat)
    through_one, gain_one_grad, bias_one_grad = norm_back(
        first_grad, normed_one, inverse_one, gain_one
    )
    input_grads = (middle_grad + through_one).reshape(images.shape) * slot_live
    small_grads = (
        gain_one_grad,
        bias_one_grad,
        qv_grad,
        out_shift_grad,
        gain_two_grad,
        bias_two_grad,
        up_shift_grad,
        down_shift_grad,
    )
    grad_table = jnp.concatenate([element.reshape(count, -1) for element in small_grads], axis=1)
    if tree:
        owned = reduce_small(grad_table)
        reduce_large = reduce_tree
    else:
        owned = lax.psum_scatter(grad_table, "dp", scatter_dimension=0, tiled=True).reshape(-1)

        def reduce_large(table):
            summed = lax.psum_scatter(table, "dp", scatter_dimension=0, tiled=True)
            return summed.astype(jnp.float32)

    down_sum = reduce_large(down_grad.astype(jnp.bfloat16)).reshape(-1)
    up_sum = reduce_large(up_grad.astype(jnp.bfloat16)).reshape(-1)
    out_sum = reduce_large(out_grad.astype(jnp.bfloat16)).reshape(-1)
    qkv_sum = reduce_large(qkv_grad.astype(jnp.bfloat16)).reshape(-1)
    pieces = []
    offset = 0
    for width in small_widths:
        pieces.append(owned[offset : offset + width])
        offset = offset + width
    return (
        outputs,
        input_grads,
        pieces[0],
        pieces[1],
        qkv_sum,
        pieces[2],
        out_sum,
        pieces[3],
        pieces[4],
        pieces[5],
        up_sum,
        pieces[6],
        down_sum,
        pieces[7],
    )


def solution(mesh):
    placed = (
        P("dp", None, None),
        P("dp"),
        P("dp"),
        P("dp"),
        P("dp"),
        P("dp"),
        P("dp"),
        P("dp"),
        P("dp"),
        P("dp"),
        P("dp"),
        P("dp"),
        P("dp"),
        P("dp"),
        P("dp", None, None),
    )
    return jax.shard_map(
        shards,
        mesh=mesh,
        in_specs=placed,
        out_specs=(
            P("dp", None, None),
            P("dp", None, None),
            P("dp"),
            P("dp"),
            P("dp"),
            P("dp"),
            P("dp"),
            P("dp"),
            P("dp"),
            P("dp"),
            P("dp"),
            P("dp"),
            P("dp"),
            P("dp"),
        ),
        check_vma=False,
    )
```
